32 devices in a mesh: group: 2 (over y), ctx: 16 (over z, x, core).
Axes of the slice: x: 2, y: 2, z: 4, core: 2. Of those that a mesh axis runs over, the one named last changes fastest.
Arguments:
- queries: bfloat16 [4096, 2048], P(('group', 'ctx')), parts along dimension 0, may hold values from -28 to 28
- fresh_kv: bfloat16 [4096, 512], P(('group', 'ctx')), parts along dimension 0, may hold values from -10 to 10
- kv_cache: bfloat16 [256, 128, 512], P(('group', 'ctx')), parts along dimension 0, may hold values from -8 to 8
- selection: int32 [32, 2], P('group'), parts along dimension 0, may hold values from 0 to 127, as said below
- ctx_lengths: int32 [4], P('group'), parts along dimension 0, may hold values from 4096 to 8192, as said below
- residual_rows: bfloat16 [2048, 2048], P(('group', 'ctx')), parts along dimension 0, may hold values from -400 to 400
- norm_gain: float32 [2048], replicated, may hold values from 0.1 to 1.9
- w_gate_up: bfloat16 [16, 2048, 1536], P('ctx'), may hold values from -0.125 to 0.125
- w_down: bfloat16 [16, 768, 2048], P('ctx'), may hold values from -0.21875 to 0.21875
- expert_ids: int32 [2048, 8], P(('group', 'ctx')), parts along dimension 0, may hold values from 0 to 15, all different within a row; in each aligned block of 64 rows (0 to 63, 64 to 127, ...) at most 40 rows name the same one
- gate_weights: float32 [2048, 8], P(('group', 'ctx')), parts along dimension 0, may hold values from 0.1 to 0.4
Outputs:
- attention: bfloat16 [4096, 2048], P(('group', 'ctx')), parts along dimension 0
- expert_out: bfloat16 [2048, 2048], P(('group', 'ctx')), parts along dimension 0
The draws below stay inside these ranges and needn't reach their ends.
There are 2 independent parts, one for each index of `group`. The reference program is written for one: setup_inputs(seed, part) draws one part's arguments, and reference() takes and returns one part's arrays. A program takes and returns all parts, laid end to end along the dimension named above; an argument that names none is the same for every part. Nothing has to cross between parts.
Inputs may be any that keep to these rules, and one draw needn't show every extreme that they name: `selection`: row r names the 2 cache blocks read by the query block of device r: blocks b of request q = r // 8, that is b mod 2 = q, with (b // 2) * 128 < ctx_lengths[q]; no two of them are held by the same device. `ctx_lengths`: entry q counts the cached tokens of request q; one of the two entries is 8192. `expert_ids`: each row names 8 different experts; the 64 tokens of one device name one expert at most 40 times, a bound that some block reaches.
All inputs are finite; a program needn't handle non-finite values.
Results may differ from the reference program's by a relative error of at most 0.007.
Values may be sent and summed in bfloat16 or wider, within the bound.
A program may use at most 128 MiB of HBM per device.

```python
import math
import jax
import jax.numpy as jnp
import numpy as np
from jax import lax

D = 2048
HEADS = 16
KV_HEADS = 2
HEAD_DIM = 128
FF = 768
TOPK = 8
BLOCK = 128
ETOK = 64
KB_DEV = 8
SEL = 2
EXPERTS = 16
CAPE = 40
ETOKENS = 1024
N_CTX = 16


def attention_parts(key):
    base = jax.random.fold_in(key, 71)
    streams = jax.random.split(base, 6)
    direction = jnp.clip(jax.random.normal(streams[0], (N_CTX, KV_HEADS, HEAD_DIM), jnp.float32), -3.0, 3.0)
    return (direction, streams)


def draw_queries(key, part):
    direction, streams = attention_parts(key)
    tokens = N_CTX * BLOCK
    groups = HEADS // KV_HEADS
    owner = jnp.arange(tokens) // BLOCK
    spread = jnp.clip(jax.random.normal(streams[2], (tokens, KV_HEADS, groups, HEAD_DIM), jnp.float32), -6.0, 6.0)
    values = 0.85 * spread + 0.5 * direction[owner][:, :, None, :]
    return values.reshape(tokens, HEADS * HEAD_DIM).astype(jnp.bfloat16)


def draw_fresh_kv(key, part):
    direction, streams = attention_parts(key)
    tokens = N_CTX * BLOCK
    owner = jnp.arange(tokens) // BLOCK
    noise = jnp.clip(jax.random.normal(streams[3], (tokens, KV_HEADS, HEAD_DIM), jnp.float32), -6.0, 6.0)
    values = jnp.clip(jax.random.normal(streams[4], (tokens, KV_HEADS * HEAD_DIM), jnp.float32), -6.0, 6.0)
    key_part = 0.85 * noise + 0.6 * direction[owner]
    return jnp.concatenate([key_part.reshape(tokens, KV_HEADS * HEAD_DIM), values], axis=1).astype(jnp.bfloat16)


def draw_kv_cache(key, part):
    blocks = N_CTX * KB_DEV
    width = KV_HEADS * HEAD_DIM
    streams = jax.random.split(jax.random.fold_in(key, 5), 4)
    key_mean = jnp.clip(jax.random.normal(streams[0], (blocks, 1, width), jnp.float32), -4.0, 4.0)
    value_mean = jnp.clip(jax.random.normal(streams[1], (blocks, 1, width), jnp.float32), -4.0, 4.0)
    key_noise = jnp.clip(jax.random.normal(streams[2], (blocks, BLOCK, width), jnp.float32), -6.0, 6.0)
    value_noise = jnp.clip(jax.random.normal(streams[3], (blocks, BLOCK, width), jnp.float32), -6.0, 6.0)
    key_part = key_mean + 0.6 * key_noise
    value_part = value_mean + 0.5 * value_noise
    return jnp.concatenate([key_part, value_part], axis=2).astype(jnp.bfloat16)


def context_plan(key):
    request_blocks = N_CTX * KB_DEV // 2
    half_dev = KB_DEV // 2
    owners = N_CTX // 2
    full = request_blocks * BLOCK
    streams = jax.random.split(jax.random.fold_in(key, 9), 4)
    longer = jax.random.randint(streams[0], (), 0, 2)
    other = jax.random.randint(streams[1], (), full // 2, full + 1)
    lengths = jnp.where(jnp.arange(2) == longer, full, other).astype(jnp.int32)
    counted = (lengths + BLOCK - 1) // BLOCK
    usable = (counted + half_dev - 1) // half_dev
    request = jnp.arange(N_CTX, dtype=jnp.int32) // owners
    columns = jnp.arange(N_CTX, dtype=jnp.int32)[None, :]
    scores = jax.random.randint(streams[2], (N_CTX, N_CTX), 0, 2 ** 20) * N_CTX + columns
    scores = jnp.where(columns < usable[request][:, None], scores, scores + 2 ** 30)
    picked = jnp.argsort(scores, axis=1)[:, :SEL].astype(jnp.int32)
    room = jnp.minimum(half_dev, counted[request][:, None] - picked * half_dev)
    extra = jax.random.randint(streams[3], (N_CTX, SEL), 0, 2 ** 20) % room
    chosen = picked * KB_DEV + 2 * extra + request[:, None]
    return (lengths, chosen.astype(jnp.int32))


def draw_selection(key, part):
    lengths, chosen = context_plan(key)
    return chosen


def draw_ctx_lengths(key, part):
    lengths, chosen = context_plan(key)
    return lengths


def draw_residual_rows(key, part):
    tokens = N_CTX * ETOK
    streams = jax.random.split(jax.random.fold_in(key, 13), 3)
    row_scale = jnp.exp(jax.random.uniform(streams[0], (tokens, 1), jnp.float32, 0.0, jnp.log(10.0)))
    column_scale = jnp.exp(jax.random.uniform(streams[1], (1, D), jnp.float32, 0.0, jnp.log(10.0)))
    values = jnp.clip(jax.random.normal(streams[2], (tokens, D), jnp.float32), -4.0, 4.0)
    return (values * row_scale * column_scale).astype(jnp.bfloat16)


def levels(key, shape, shards, least, high):
    loudness = 1.0
    for dim, shards_of in shards:
        draws = jax.random.uniform(jax.random.fold_in(jax.random.fold_in(key, 6), dim), (shards_of,), jnp.float32, least / len(shards), high / len(shards))
        loudness = loudness * jnp.repeat(jnp.exp(draws), shape[dim] // shards_of).reshape((-1,) + (1,) * (len(shape) - 1 - dim))
    return loudness


def deal_out(stream_key, own, number, rows, number_of, top, most, slope):
    order = jax.random.permutation(stream_key, number_of)
    crowded, usual = shares(number_of, rows * top, most, slope, True), shares(number_of, rows * top, most, slope, False)
    places = jnp.arange(number_of)

    def named(tallies, rotation):
        used = int((tallies > 0).sum())
        fixed = max(1, used // 4)
        passed = fixed + (places - fixed + rotation * (used - fixed)) % max(1, number_of - fixed)
        return jnp.zeros((number_of,), jnp.int32).at[order[jnp.where(places < fixed, places, passed)]].set(jnp.asarray(tallies, jnp.int32))

    tallies = jnp.where(number % 4 == 0, named(crowded, number // 4), named(usual, number - number // 4 - 1))
    mixed = jax.random.permutation(jax.random.fold_in(own, 3), number_of)
    source_of, sink = mixed[0:number_of // 2 * 2:2], mixed[1:number_of // 2 * 2:2]
    margin = jnp.minimum(tallies[source_of] - 1, most - tallies[sink]) // 2
    margin = jnp.where((source_of == order[0]) | (sink == order[0]) | (tallies[sink] == 0), 0, jnp.maximum(margin, 0))
    passed = jax.random.randint(jax.random.fold_in(own, 4), (number_of // 2,), 0, 1 << 20) % (margin + 1)
    tallies = tallies.at[source_of].add(-passed).at[sink].add(passed)
    members = jnp.searchsorted(jnp.cumsum(tallies), jnp.arange(rows * top), side="right").astype(jnp.int32)
    grid = members.reshape(top, rows).T
    grid = grid[jax.random.permutation(jax.random.fold_in(own, 1), rows)]
    rotation = jax.random.randint(jax.random.fold_in(own, 2), (rows, 1), 0, top)
    return jnp.take_along_axis(grid, (jnp.arange(top)[None, :] + rotation) % top, axis=1)


def shares(count, total, most, slope, full):
    portions = [(1 << 20) // math.isqrt(rank ** slope) + 1 for rank in range(1, count + 1)]
    largest = most if full else min(most, max(-(-total // count), total * portions[0] // sum(portions)))
    least = 1 if total - largest >= count - 1 else 0
    given, rest = [largest] + [least] * (count - 1), total - largest - least * (count - 1)
    while rest > 0:
        candidates = [i for i in range(1, count) if given[i] < largest] or [i for i in range(1, count) if given[i] < most]
        mass, remaining = sum([portions[i] for i in candidates]), rest
        for i in candidates:
            more = min(most - given[i], max(1, remaining * portions[i] // mass), rest)
            given[i] = given[i] + more
            rest = rest - more
    return np.array(given)


def normal_values(rng, extent, deviation, limit, cuts=(), kind=jnp.bfloat16):
    result = jax.random.normal(rng, extent, jnp.float32) * deviation
    if len(cuts) > 0:
        result = levels(rng, extent, cuts, -0.22, 0.18) * result
    return jnp.clip(result, min=-limit, max=limit).astype(kind)


def setup_inputs(seed: int = 0, part: int = 0) -> dict:
    key_of = jax.random.split(jax.random.key(seed), 12)
    part_splits = jax.random.split(jax.random.fold_in(key_of[11], part), 12)
    queries = draw_queries(jax.random.fold_in(jax.random.fold_in(key_of[11], part), 71), part)
    fresh_kv = draw_fresh_kv(jax.random.fold_in(jax.random.fold_in(key_of[11], part), 71), part)
    kv_cache = draw_kv_cache(jax.random.fold_in(jax.random.fold_in(key_of[11], part), 71), part)
    selection = draw_selection(jax.random.fold_in(jax.random.fold_in(key_of[11], part), 71), part)
    ctx_lengths = draw_ctx_lengths(jax.random.fold_in(jax.random.fold_in(key_of[11], part), 71), part)
    residual_rows = draw_residual_rows(jax.random.fold_in(jax.random.fold_in(key_of[11], part), 71), part)
    norm_gain = jnp.clip(1.0 + 0.18 * jax.random.normal(key_of[6], (D,), jnp.float32), 0.1, 1.9)
    w_gate_up = normal_values(key_of[7], (EXPERTS, D, 2 * FF), D ** -0.5, 0.125, ((0, 16),))
    w_down = normal_values(key_of[8], (EXPERTS, FF, D), FF ** -0.5, 0.21875, ((0, 16),))
    expert_ids_keys = jax.random.split(jax.random.fold_in(part_splits[9], 1), ETOKENS // ETOK)
    expert_ids_turns = jax.random.permutation(jax.random.fold_in(part_splits[9], 3), ETOKENS // ETOK)
    expert_ids = jax.vmap(lambda own, number: deal_out(jax.random.fold_in(part_splits[9], 2), own, number, ETOK, EXPERTS, TOPK, CAPE, 2))(expert_ids_keys, expert_ids_turns).reshape((ETOKENS, TOPK))
    gate_weights = jnp.clip(0.1 + 0.3 * jax.random.uniform(part_splits[10], (ETOKENS, TOPK), jnp.float32) ** levels(part_splits[10], (ETOKENS, TOPK), ((0, 16),), -0.2, 0.2), 0.1, 0.4)
    return dict(queries=queries, fresh_kv=fresh_kv, kv_cache=kv_cache, selection=selection, ctx_lengths=ctx_lengths, residual_rows=residual_rows, norm_gain=norm_gain, w_gate_up=w_gate_up, w_down=w_down, expert_ids=expert_ids, gate_weights=gate_weights)


masked_score = -1e+30
epsilon = 1e-06

def rms_normed(hidden_rows, gain_row):
    values = hidden_rows.astype(jnp.float32)
    mean_square = lax.optimization_barrier(jnp.mean(values * values, axis=-1, keepdims=True))
    return (values * lax.rsqrt(mean_square + epsilon) * gain_row.astype(jnp.float32)).astype(jnp.bfloat16)

def key_usable(chosen, ctx_lengths):
    request = chosen % 2
    within = chosen // 2
    limits = jnp.take(ctx_lengths, request)
    position = within[:, None] * BLOCK + jnp.arange(BLOCK, dtype=jnp.int32)[None, :]
    return (position < limits[:, None]).reshape(-1)

def attend_block(queried, kv_rows, usable_mask):
    groups = HEADS // KV_HEADS
    shaped = queried.astype(jnp.float32).reshape(BLOCK, KV_HEADS, groups, HEAD_DIM)
    key_part = kv_rows[:, :KV_HEADS * HEAD_DIM].astype(jnp.float32).reshape(-1, KV_HEADS, HEAD_DIM)
    value_part = kv_rows[:, KV_HEADS * HEAD_DIM:].astype(jnp.float32).reshape(-1, KV_HEADS, HEAD_DIM)
    scores = jnp.einsum('tkgd,lkd->kgtl', shaped, key_part, precision=lax.Precision.HIGHEST) * HEAD_DIM ** (-0.5)
    scores = jnp.where(usable_mask[None, None], scores, masked_score)
    largest = lax.optimization_barrier(jnp.max(scores, axis=-1, keepdims=True))
    weights = jnp.exp(scores - largest)
    totals = lax.optimization_barrier(jnp.sum(weights, axis=-1))
    rounded = lax.optimization_barrier(weights.astype(jnp.bfloat16)).astype(jnp.float32)
    blended = jnp.einsum('kgtl,lkd->tkgd', rounded, value_part, precision=lax.Precision.HIGHEST)
    blended = blended / jnp.transpose(totals, (2, 0, 1))[..., None]
    return blended.reshape(BLOCK, HEADS * HEAD_DIM).astype(jnp.bfloat16)

def slot_tables(expert_ids, gate_weights, experts, capacity):
    flat_ids = expert_ids.reshape(-1)
    one_hot = (flat_ids[:, None] == jnp.arange(experts, dtype=jnp.int32)[None, :]).astype(jnp.int32)
    earlier = jnp.cumsum(one_hot, axis=0) - one_hot
    slot_rank = lax.optimization_barrier(jnp.sum(earlier * one_hot, axis=1))
    placement = flat_ids * capacity + slot_rank
    amount = expert_ids.shape[0] * expert_ids.shape[1]
    owner_token = jnp.arange(amount, dtype=jnp.int32) // expert_ids.shape[1]
    token_table = jnp.zeros((experts * capacity,), jnp.int32).at[placement].set(owner_token)
    filled = jnp.zeros((experts * capacity,), jnp.int32).at[placement].set(1)
    gate_table = jnp.zeros((experts * capacity,), jnp.float32).at[placement].set(gate_weights.reshape(-1))
    return (token_table, filled, gate_table)

def expert_rows(token_rows, gate_up, down_proj):
    gate_and_up = jnp.dot(token_rows, gate_up, preferred_element_type=jnp.float32)
    hidden_units = down_proj.shape[0]
    active = (jax.nn.silu(gate_and_up[:, :hidden_units]) * gate_and_up[:, hidden_units:]).astype(jnp.bfloat16)
    return jnp.dot(active, down_proj, preferred_element_type=jnp.float32).astype(jnp.bfloat16)

def reference(queries, fresh_kv, kv_cache, selection, ctx_lengths, residual_rows, norm_gain, w_gate_up, w_down, expert_ids, gate_weights):
    causal = jnp.arange(BLOCK)[:, None] >= jnp.arange(BLOCK)[None, :]

    def one_block(device):
        queried = lax.dynamic_slice_in_dim(queries, device * BLOCK, BLOCK, 0)
        own_rows = lax.dynamic_slice_in_dim(fresh_kv, device * BLOCK, BLOCK, 0)
        chosen = lax.dynamic_index_in_dim(selection, device, 0, keepdims=False)
        blocks = jnp.take(kv_cache, chosen, axis=0)
        kv_rows = jnp.concatenate([blocks.reshape(-1, blocks.shape[2]), own_rows], axis=0)
        usable = key_usable(chosen, ctx_lengths)
        usable_mask = jnp.concatenate([jnp.broadcast_to(usable[None, :], (BLOCK, usable.shape[0])), causal], axis=1)
        return attend_block(queried, kv_rows, usable_mask)
    attention = lax.map(one_block, jnp.arange(N_CTX, dtype=jnp.int32)).reshape(N_CTX * BLOCK, HEADS * HEAD_DIM)
    normed = rms_normed(residual_rows, norm_gain)
    ids_blocks = expert_ids.reshape(N_CTX, ETOK, TOPK)
    gate_blocks = gate_weights.reshape(N_CTX, ETOK, TOPK)
    token_table, filled, gate_table = jax.vmap(lambda ids_row, gates_row: slot_tables(ids_row, gates_row, N_CTX, CAPE))(ids_blocks, gate_blocks)
    offsets = jnp.arange(N_CTX, dtype=jnp.int32)[:, None] * ETOK
    global_table = (token_table + offsets).reshape(N_CTX, N_CTX, CAPE)
    filled_table = filled.reshape(N_CTX, N_CTX, CAPE)
    gate_slots = gate_table.reshape(N_CTX, N_CTX, CAPE)

    def one_expert(accumulated, inputs):
        gate_up, down_proj, tokens_in, filled_in, gates_in = inputs
        token_index = tokens_in.reshape(-1)
        token_rows = jnp.where(filled_in.reshape(-1)[:, None] > 0, jnp.take(normed, token_index, axis=0), 0)
        produced = expert_rows(token_rows, gate_up, down_proj).astype(jnp.float32)
        scaled = produced * gates_in.reshape(-1)[:, None]
        return (accumulated.at[token_index].add(scaled), None)
    inputs = (w_gate_up, w_down, jnp.transpose(global_table, (1, 0, 2)), jnp.transpose(filled_table, (1, 0, 2)), jnp.transpose(gate_slots, (1, 0, 2)))
    accumulated, ignored = lax.scan(one_expert, jnp.zeros((N_CTX * ETOK, D), jnp.float32), inputs)
    return (attention, accumulated.astype(jnp.bfloat16))
```

```python
import jax
import jax.numpy as jnp
from jax import lax
from jax.sharding import PartitionSpec as P

HEADS = 16
KV_HEADS = 2
HEAD_DIM = 128
TOPK = 8
BLOCK = 128


masked_score = -1e30
epsilon = 1e-06


def rms_normed(hidden_rows, gain_row):
    values = hidden_rows.astype(jnp.float32)
    mean_square = jnp.mean(values * values, axis=-1, keepdims=True)
    return (values * lax.rsqrt(mean_square + epsilon) * gain_row).astype(jnp.bfloat16)


def key_usable(chosen, ctx_lengths):
    request = chosen % 2
    within = chosen // 2
    limits = jnp.take(ctx_lengths, request)
    position = within[:, None] * BLOCK + jnp.arange(BLOCK, dtype=jnp.int32)[None, :]
    return (position < limits[:, None]).reshape(-1)


def head_scores(queried, kv_rows, usable_mask, kv_head):
    offset = kv_head * HEAD_DIM
    key_part = kv_rows[:, offset : offset + HEAD_DIM]
    value_start = (KV_HEADS + kv_head) * HEAD_DIM
    value_part = kv_rows[:, value_start : value_start + HEAD_DIM]
    scores = jnp.einsum(
        "tgd,ld->gtl", queried[:, kv_head], key_part, preferred_element_type=jnp.float32
    ) * HEAD_DIM ** (-0.5)
    return (jnp.where(usable_mask[None], scores, masked_score), value_part)


def attend_rows(queried, kv_rows, usable_mask):
    pieces_out = []
    for kv_head in range(KV_HEADS):
        scores, value_part = head_scores(queried, kv_rows, usable_mask, kv_head)
        largest = jnp.max(scores, axis=-1, keepdims=True)
        weights = jnp.exp(scores - largest)
        totals = jnp.sum(weights, axis=-1)
        blended = jnp.einsum(
            "gtl,ld->tgd",
            weights.astype(jnp.bfloat16),
            value_part,
            preferred_element_type=jnp.float32,
        )
        pieces_out.append(blended / jnp.transpose(totals)[:, :, None])
    return jnp.stack(pieces_out, axis=1)


def attention_layer(queries, fresh_kv, kv_cache, selection, ctx_lengths):
    device_index = lax.axis_index("ctx")
    stored = kv_cache.shape[0]
    tokens = queries.shape[0]
    groups = HEADS // KV_HEADS
    queried = queries.reshape(tokens, KV_HEADS, groups, HEAD_DIM)
    chosen_blocks = lax.dynamic_index_in_dim(selection, device_index, 0, keepdims=False)
    causal = jnp.arange(tokens)[:, None] >= jnp.arange(tokens)[None, :]
    wanted = selection // stored == device_index
    if lax.axis_size("ctx") <= 2 * TOPK:
        outgoing = jnp.where(
            wanted[:, :, None, None], jnp.take(kv_cache, selection % stored, axis=0), 0
        )
        blocks = lax.psum_scatter(outgoing, "ctx", scatter_dimension=0, tiled=True)[0]
        return attend(queried, blocks, fresh_kv, chosen_blocks, ctx_lengths, causal)
    local_index = jnp.sum(jnp.where(wanted, selection % stored, 0), axis=1)
    asked = jnp.any(wanted, axis=1)
    outgoing = jnp.where(asked[:, None, None], jnp.take(kv_cache, local_index, axis=0), 0)
    arrived = lax.all_to_all(outgoing, "ctx", split_axis=0, concat_axis=0, tiled=True)
    blocks = jnp.take(arrived, chosen_blocks // stored, axis=0)
    return attend(queried, blocks, fresh_kv, chosen_blocks, ctx_lengths, causal)


def attend(queried, blocks, fresh_kv, chosen_blocks, ctx_lengths, causal):
    tokens = queried.shape[0]
    kv_rows = jnp.concatenate([blocks.reshape(-1, blocks.shape[2]), fresh_kv], axis=0)
    usable = key_usable(chosen_blocks, ctx_lengths)
    usable_mask = jnp.concatenate(
        [jnp.broadcast_to(usable[None, :], (tokens, usable.shape[0])), causal], axis=1
    )
    blended = attend_rows(queried, kv_rows, usable_mask)
    return blended.reshape(tokens, HEADS * HEAD_DIM).astype(jnp.bfloat16)


def slot_places(expert_ids, experts, capacity):
    flat_ids = expert_ids.reshape(-1)
    one_hot = (flat_ids[:, None] == jnp.arange(experts, dtype=jnp.int32)[None, :]).astype(jnp.int32)
    earlier = jnp.cumsum(one_hot, axis=0) - one_hot
    slot_rank = jnp.sum(earlier * one_hot, axis=1)
    placement = flat_ids * capacity + slot_rank
    amount = expert_ids.shape[0] * expert_ids.shape[1]
    owner_token = jnp.arange(amount, dtype=jnp.int32) // expert_ids.shape[1]
    token_table = jnp.zeros((experts * capacity,), jnp.int32).at[placement].set(owner_token)
    filled = jnp.zeros((experts * capacity,), jnp.int32).at[placement].set(1)
    return (placement, token_table, filled)


def expert_rows(token_rows, gate_up, down_proj):
    gate_and_up = jnp.dot(token_rows, gate_up, preferred_element_type=jnp.float32)
    hidden_units = down_proj.shape[0]
    active = (jax.nn.silu(gate_and_up[:, :hidden_units]) * gate_and_up[:, hidden_units:]).astype(
        jnp.bfloat16
    )
    return jnp.dot(active, down_proj, preferred_element_type=jnp.float32).astype(jnp.bfloat16)


def dense_experts(normed, gate_up, down_proj, expert_ids, gate_weights):
    experts = lax.axis_size("ctx")
    columns = jnp.arange(experts, dtype=jnp.int32)
    named = expert_ids[:, :, None] == columns[None, None, :]
    gates = jnp.sum(jnp.where(named, gate_weights[:, :, None], 0.0), axis=1)
    gates = lax.all_to_all(gates.T.reshape(experts, -1), "ctx", 0, 0, tiled=True).reshape(-1)
    rows = lax.all_gather(normed, "ctx", axis=0, tiled=True)
    produced = expert_rows(rows, gate_up, down_proj).astype(jnp.float32)
    scaled = jnp.where(gates[:, None] > 0, produced * gates[:, None], 0.0).astype(jnp.bfloat16)
    return lax.psum_scatter(scaled, "ctx", scatter_dimension=0, tiled=True)


def expert_layer(residual_rows, norm_gain, w_gate_up, w_down, expert_ids, gate_weights):
    experts = lax.axis_size("ctx")
    capacity = max(3, 5 * expert_ids.shape[0] * TOPK // (4 * experts))
    normed = rms_normed(residual_rows, norm_gain)
    if experts <= 2 * TOPK:
        return dense_experts(normed, w_gate_up[0], w_down[0], expert_ids, gate_weights)
    placement, token_table, filled = slot_places(expert_ids, experts, capacity)
    outgoing = jnp.where(filled[:, None] > 0, jnp.take(normed, token_table, axis=0), 0)
    outgoing = outgoing.reshape(experts, capacity, normed.shape[1])
    arrived = lax.all_to_all(outgoing, "ctx", split_axis=0, concat_axis=0, tiled=True)
    amount = arrived.shape[1]
    produced = expert_rows(arrived.reshape(-1, arrived.shape[2]), w_gate_up[0], w_down[0])
    returned = lax.all_to_all(
        produced.reshape(experts, amount, produced.shape[1]),
        "ctx",
        split_axis=0,
        concat_axis=0,
        tiled=True,
    )
    picked = jnp.take(
        returned.reshape(experts * capacity, returned.shape[2]), placement, axis=0
    ).astype(jnp.float32)
    picked = picked * gate_weights.reshape(-1)[:, None]
    summed = jnp.sum(
        picked.reshape(expert_ids.shape[0], expert_ids.shape[1], picked.shape[1]), axis=1
    )
    return summed.astype(jnp.bfloat16)


def shards(
    queries,
    fresh_kv,
    kv_cache,
    selection,
    ctx_lengths,
    residual_rows,
    norm_gain,
    w_gate_up,
    w_down,
    expert_ids,
    gate_weights,
):
    attention = attention_layer(queries, fresh_kv, kv_cache, selection, ctx_lengths)
    expert_out = expert_layer(residual_rows, norm_gain, w_gate_up, w_down, expert_ids, gate_weights)
    return (attention, expert_out)


def solution(mesh):
    return jax.shard_map(
        shards,
        mesh=mesh,
        in_specs=(
            P(("group", "ctx"), None),
            P(("group", "ctx"), None),
            P(("group", "ctx"), None, None),
            P("group", None),
            P("group"),
            P(("group", "ctx"), None),
            P(),
            P("ctx", None, None),
            P("ctx", None, None),
            P(("group", "ctx"), None),
            P(("group", "ctx"), None),
        ),
        out_specs=(P(("group", "ctx"), None), P(("group", "ctx"), None)),
        check_vma=False,
    )
```

```python
import functools

import jax
import jax.numpy as jnp
from jax import lax
from jax.experimental import pallas as pl
from jax.experimental.pallas import tpu as pltpu
from jax.sharding import PartitionSpec as P

HEADS = 16
KV_HEADS = 2
HEAD_DIM = 128
TOPK = 8
BLOCK = 128


masked_score = -1e30
epsilon = 1e-06


def rms_normed(hidden_rows, gain_row):
    values = hidden_rows.astype(jnp.float32)
    mean_square = jnp.mean(values * values, axis=-1, keepdims=True)
    return (values * lax.rsqrt(mean_square + epsilon) * gain_row).astype(jnp.bfloat16)


def key_usable(chosen, ctx_lengths):
    request = chosen % 2
    within = chosen // 2
    limits = jnp.take(ctx_lengths, request)
    position = within[:, None] * BLOCK + jnp.arange(BLOCK, dtype=jnp.int32)[None, :]
    return (position < limits[:, None]).reshape(-1)


def head_scores(queried, kv_rows, usable_mask, kv_head):
    offset = kv_head * HEAD_DIM
    key_part = kv_rows[:, offset : offset + HEAD_DIM]
    value_start = (KV_HEADS + kv_head) * HEAD_DIM
    value_part = kv_rows[:, value_start : value_start + HEAD_DIM]
    scores = jnp.einsum(
        "tgd,ld->gtl", queried[:, kv_head], key_part, preferred_element_type=jnp.float32
    ) * HEAD_DIM ** (-0.5)
    return (jnp.where(usable_mask[None], scores, masked_score), value_part)


def attend_rows(queried, kv_rows, usable_mask):
    pieces_out = []
    for kv_head in range(KV_HEADS):
        scores, value_part = head_scores(queried, kv_rows, usable_mask, kv_head)
        largest = jnp.max(scores, axis=-1, keepdims=True)
        weights = jnp.exp(scores - largest)
        totals = jnp.sum(weights, axis=-1)
        blended = jnp.einsum(
            "gtl,ld->tgd",
            weights.astype(jnp.bfloat16),
            value_part,
            preferred_element_type=jnp.float32,
        )
        pieces_out.append(blended / jnp.transpose(totals)[:, :, None])
    return jnp.stack(pieces_out, axis=1)


def attention_layer(queries, fresh_kv, kv_cache, selection, ctx_lengths):
    device_index = lax.axis_index("ctx")
    stored = kv_cache.shape[0]
    tokens = queries.shape[0]
    groups = HEADS // KV_HEADS
    queried = queries.reshape(tokens, KV_HEADS, groups, HEAD_DIM)
    chosen_blocks = lax.dynamic_index_in_dim(selection, device_index, 0, keepdims=False)
    causal = jnp.arange(tokens)[:, None] >= jnp.arange(tokens)[None, :]
    wanted = selection // stored == device_index
    local_index = jnp.sum(jnp.where(wanted, selection % stored, 0), axis=1)
    asked = jnp.any(wanted, axis=1)
    outgoing = jnp.where(asked[:, None, None], jnp.take(kv_cache, local_index, axis=0), 0)
    arrived = lax.all_to_all(outgoing, "ctx", split_axis=0, concat_axis=0, tiled=True)
    blocks = jnp.take(arrived, chosen_blocks // stored, axis=0)
    return attend(queried, blocks, fresh_kv, chosen_blocks, ctx_lengths, causal)


def attend(queried, blocks, fresh_kv, chosen_blocks, ctx_lengths, causal):
    tokens = queried.shape[0]
    kv_rows = jnp.concatenate([blocks.reshape(-1, blocks.shape[2]), fresh_kv], axis=0)
    usable = key_usable(chosen_blocks, ctx_lengths)
    usable_mask = jnp.concatenate(
        [jnp.broadcast_to(usable[None, :], (tokens, usable.shape[0])), causal], axis=1
    )
    blended = attend_rows(queried, kv_rows, usable_mask)
    return blended.reshape(tokens, HEADS * HEAD_DIM).astype(jnp.bfloat16)


def slot_places(expert_ids, experts, capacity):
    flat_ids = expert_ids.reshape(-1)
    one_hot = (flat_ids[:, None] == jnp.arange(experts, dtype=jnp.int32)[None, :]).astype(jnp.int32)
    earlier = jnp.cumsum(one_hot, axis=0) - one_hot
    slot_rank = jnp.sum(earlier * one_hot, axis=1)
    placement = flat_ids * capacity + slot_rank
    amount = expert_ids.shape[0] * expert_ids.shape[1]
    owner_token = jnp.arange(amount, dtype=jnp.int32) // expert_ids.shape[1]
    token_table = jnp.zeros((experts * capacity,), jnp.int32).at[placement].set(owner_token)
    filled = jnp.zeros((experts * capacity,), jnp.int32).at[placement].set(1)
    return (placement, token_table, filled)


def expert_rows(token_rows, gate_up, down_proj):
    gate_and_up = jnp.dot(token_rows, gate_up, preferred_element_type=jnp.float32)
    hidden_units = down_proj.shape[0]
    active = (jax.nn.silu(gate_and_up[:, :hidden_units]) * gate_and_up[:, hidden_units:]).astype(
        jnp.bfloat16
    )
    return jnp.dot(active, down_proj, preferred_element_type=jnp.float32).astype(jnp.bfloat16)


def expert_layer(residual_rows, norm_gain, w_gate_up, w_down, expert_ids, gate_weights):
    experts = lax.axis_size("ctx")
    capacity = max(3, 5 * expert_ids.shape[0] * TOPK // (4 * experts))
    normed = rms_normed(residual_rows, norm_gain)
    placement, token_table, filled = slot_places(expert_ids, experts, capacity)
    outgoing = jnp.where(filled[:, None] > 0, jnp.take(normed, token_table, axis=0), 0)
    outgoing = outgoing.reshape(experts, capacity, normed.shape[1])
    arrived = lax.all_to_all(outgoing, "ctx", split_axis=0, concat_axis=0, tiled=True)
    amount = arrived.shape[1]
    produced = expert_rows(arrived.reshape(-1, arrived.shape[2]), w_gate_up[0], w_down[0])
    returned = lax.all_to_all(
        produced.reshape(experts, amount, produced.shape[1]),
        "ctx",
        split_axis=0,
        concat_axis=0,
        tiled=True,
    )
    picked = jnp.take(
        returned.reshape(experts * capacity, returned.shape[2]), placement, axis=0
    ).astype(jnp.float32)
    picked = picked * gate_weights.reshape(-1)[:, None]
    summed = jnp.sum(
        picked.reshape(expert_ids.shape[0], expert_ids.shape[1], picked.shape[1]), axis=1
    )
    return summed.astype(jnp.bfloat16)


MESH = pl.DeviceIdType.MESH


class Ring:
    def __init__(self, count):
        self.chips = count // 2
        self.rows = self.chips // 2
        me = lax.axis_index("ctx")
        self.core = me % 2
        chip = me // 2
        level, column = chip // 2, chip % 2
        self.place = level + column * (self.chips - 1 - 2 * level)
        self.near = self.half()
        self.used = 0

    def half(self):
        far = self.chips // 2
        return ((far, self.chips - 1 - far), (self.chips - 1 - far, far))

    def device(self, offset, core):
        place = (self.place + offset + self.chips) % self.chips
        column = place // self.rows
        level = place + column * (self.chips - 1 - 2 * place)
        return (level * 2 + column) * 2 + core

    def copy(self, source, target, sems, device):
        send, recv = sems
        index = self.used
        self.used += 1
        return pltpu.make_async_remote_copy(
            src_ref=source,
            dst_ref=target,
            send_sem=send.at[index],
            recv_sem=recv.at[index],
            device_id={"ctx": device},
            device_id_type=MESH,
        )

    def greet(self):
        barrier = pltpu.get_barrier_semaphore()
        for device in self.partners():
            pl.semaphore_signal(barrier, inc=1, device_id={"ctx": device}, device_id_type=MESH)
        pl.semaphore_wait(barrier, 3)

    def partners(self):
        return (
            self.device(0, 1 - self.core),
            self.device(1, self.core),
            self.device(-1, self.core),
        )


class Gather:
    def __init__(self, ring, sems, source, target, pieces):
        self.ring, self.sems, self.source, self.target = ring, sems, source, target
        self.pieces = pieces
        self.ways = {}
        self.aside = []

    def across(self, view, index):
        ring = self.ring
        copy = ring.copy(
            view, self.target.at[index], self.sems, ring.device(0, 1 - ring.core)
        )
        copy.start()
        self.aside.append(copy)

    def step(self, number):
        ring = self.ring
        for at, (start, rows, lengths) in enumerate(self.pieces):
            for side, length in zip((1, -1), lengths):
                key = (at, side)
                span = pl.ds(start, rows)
                origin = ring.device(-side * number, ring.core)
                if 0 < number <= length:
                    self.ways[key][-1].wait_recv()
                if number < length:
                    view = self.source.at[span] if number == 0 else self.target.at[origin, span]
                    copy = ring.copy(
                        view, self.target.at[origin, span], self.sems, ring.device(side, ring.core)
                    )
                    copy.start()
                    self.ways.setdefault(key, []).append(copy)
                if 0 < number <= length:
                    self.across(self.target.at[origin, span], (origin, span))
        if number == 0:
            me = ring.device(0, ring.core)
            self.across(self.source, me)
            self.target[me] = self.source[...]

    def finish(self):
        for copy in self.aside:
            copy.wait()
        for copies in self.ways.values():
            for copy in copies:
                copy.wait_send()


class Scatter:
    def __init__(self, ring, sems, source, target, other, sent, got):
        self.ring, self.sems, self.source, self.target = ring, sems, source, target
        self.other, self.sent, self.got = other, sent, got
        self.rows = source.shape[1] // 2
        self.ways, self.used = {}, 0
        self.aside = {}

    def begin(self):
        ring = self.ring
        far = ring.chips // 2
        order = [far]
        for near in range(far - 1, 0, -1):
            order += [near, ring.chips - near]
        order.append(0)
        for offset in order:
            copy = ring.copy(
                self.source.at[ring.device(offset, 1 - ring.core)],
                self.other.at[offset],
                self.sems,
                ring.device(0, 1 - ring.core),
            )
            copy.start()
            self.aside[offset] = [copy, False]

    def local(self, offset, span):
        offset = offset % self.ring.chips
        copy, seen = self.aside[offset]
        if not seen:
            copy.wait_recv()
            self.aside[offset][1] = True
        own = self.source[self.ring.device(offset, self.ring.core), span]
        return own.astype(jnp.float32) + self.other[offset, span].astype(jnp.float32)

    def step(self, number):
        ring = self.ring
        for at, lengths in enumerate(ring.near):
            span = pl.ds(at * self.rows, self.rows)
            for side, length in zip((1, -1), lengths):
                if number >= length:
                    continue
                value = self.local(side * (length - number), span)
                if number > 0:
                    before = self.ways[at, side][-1]
                    before[0].wait_recv()
                    value = value + self.got[before[1]].astype(jnp.float32)
                slot = self.used
                self.used += 1
                self.sent[slot] = value.astype(self.sent.dtype)
                copy = ring.copy(
                    self.sent.at[slot], self.got.at[slot], self.sems, ring.device(side, ring.core)
                )
                copy.start()
                self.ways.setdefault((at, side), []).append((copy, slot))

    def finish(self):
        for at in range(2):
            span = pl.ds(at * self.rows, self.rows)
            value = self.local(0, span)
            for side in (1, -1):
                copy, slot = self.ways[at, side][-1]
                copy.wait_recv()
                value = value + self.got[slot].astype(jnp.float32)
            self.target[span] = value.astype(self.target.dtype)
        for copy, seen in self.aside.values():
            copy.wait_send()
        for copies in self.ways.values():
            for copy, slot in copies:
                copy.wait_send()


def scatter_scratch(count, slots):
    chips = count // 2
    hops = 2 * (chips - 1)
    rows, columns = slots.shape[1:]
    return [
        pltpu.VMEM((chips, rows, columns), slots.dtype),
        pltpu.VMEM((hops, rows // 2, columns), slots.dtype),
        pltpu.VMEM((hops, rows // 2, columns), slots.dtype),
    ], chips + hops


def first_kernel(count, rows_ref, gates_ref, slots_ref, all_rows, all_gates, kept, *scratch):
    other, sent, got, send, recv = scratch
    ring = Ring(count)
    ring.greet()
    sems = (send, recv)
    half = rows_ref.shape[0] // 2
    pieces = [(at * half, half, lengths) for at, lengths in enumerate(ring.near)]
    gates = Gather(ring, sems, gates_ref, all_gates, [(0, gates_ref.shape[0], ring.near[0])])
    rows = Gather(ring, sems, rows_ref, all_rows, pieces)
    slots = Scatter(ring, sems, slots_ref, kept, other, sent, got)
    slots.begin()
    for number in range(ring.chips // 2 + 1):
        gates.step(number)
        rows.step(number)
        slots.step(number)
    slots.finish()
    gates.finish()
    rows.finish()


def first_exchange(normed, gates, slots):
    count = lax.axis_size("ctx")
    scratch, sems = scatter_scratch(count, slots)
    chips = count // 2
    sems += 2 * 2 * (chips - 1) + 1 + 2 * (chips - 1) + 1
    vmem = pl.BlockSpec(memory_space=pltpu.VMEM)
    return pl.pallas_call(
        functools.partial(first_kernel, count),
        out_shape=(
            jax.ShapeDtypeStruct((count,) + normed.shape, normed.dtype),
            jax.ShapeDtypeStruct((count,) + gates.shape, gates.dtype),
            jax.ShapeDtypeStruct(slots.shape[1:], slots.dtype),
        ),
        in_specs=[vmem] * 3,
        out_specs=(vmem,) * 3,
        scratch_shapes=scratch
        + [pltpu.SemaphoreType.DMA((sems,)), pltpu.SemaphoreType.DMA((sems,))],
        compiler_params=pltpu.CompilerParams(collective_id=0, has_side_effects=True),
    )(normed, gates, slots)


def last_kernel(count, slots_ref, kept, other, sent, got, send, recv):
    ring = Ring(count)
    ring.greet()
    slots = Scatter(ring, (send, recv), slots_ref, kept, other, sent, got)
    slots.begin()
    for number in range(ring.chips // 2):
        slots.step(number)
    slots.finish()


def last_exchange(slots):
    count = lax.axis_size("ctx")
    scratch, sems = scatter_scratch(count, slots)
    vmem = pl.BlockSpec(memory_space=pltpu.VMEM)
    return pl.pallas_call(
        functools.partial(last_kernel, count),
        out_shape=jax.ShapeDtypeStruct(slots.shape[1:], slots.dtype),
        in_specs=[vmem],
        out_specs=vmem,
        scratch_shapes=scratch
        + [pltpu.SemaphoreType.DMA((sems,)), pltpu.SemaphoreType.DMA((sems,))],
        compiler_params=pltpu.CompilerParams(collective_id=1, has_side_effects=True),
    )(slots)


def few_devices(queries, fresh_kv, kv_cache, selection, ctx_lengths, residual_rows, norm_gain,
                w_gate_up, w_down, expert_ids, gate_weights):
    experts = lax.axis_size("ctx")
    me = lax.axis_index("ctx")
    stored = kv_cache.shape[0]
    tokens = queries.shape[0]
    local = expert_ids.shape[0]
    normed = rms_normed(residual_rows, norm_gain)
    named = expert_ids[:, :, None] == jnp.arange(experts, dtype=jnp.int32)[None, None, :]
    gates = jnp.sum(jnp.where(named, gate_weights[:, :, None], 0.0), axis=1)
    wanted = selection // stored == me
    slots = jnp.where(wanted[:, :, None, None], jnp.take(kv_cache, selection % stored, axis=0), 0)
    slots = slots.reshape(experts, -1, kv_cache.shape[2])
    rows, all_gates, blocks = first_exchange(normed, gates.reshape(-1, 128), slots)
    all_gates = all_gates.reshape(experts * local, experts)
    mine = jnp.arange(experts, dtype=jnp.int32)[None, :] == me
    gate = jnp.sum(jnp.where(mine, all_gates, 0.0), axis=1)
    produced = expert_rows(rows.reshape(experts * local, -1), w_gate_up[0], w_down[0])
    scaled = (produced.astype(jnp.float32) * gate[:, None]).astype(jnp.bfloat16)
    expert_out = last_exchange(scaled.reshape(experts, local, -1))
    queried = queries.reshape(tokens, KV_HEADS, HEADS // KV_HEADS, HEAD_DIM)
    chosen_blocks = lax.dynamic_index_in_dim(selection, me, 0, keepdims=False)
    causal = jnp.arange(tokens)[:, None] >= jnp.arange(tokens)[None, :]
    blocks = blocks.reshape(-1, BLOCK, blocks.shape[1])
    attention = attend(queried, blocks, fresh_kv, chosen_blocks, ctx_lengths, causal)
    return (attention, expert_out)


def shards(
    queries,
    fresh_kv,
    kv_cache,
    selection,
    ctx_lengths,
    residual_rows,
    norm_gain,
    w_gate_up,
    w_down,
    expert_ids,
    gate_weights,
):
    count = lax.axis_size("ctx")
    if 8 <= count <= 2 * TOPK and count % 4 == 0 and expert_ids.shape[0] * count % 1024 == 0:
        return few_devices(
            queries, fresh_kv, kv_cache, selection, ctx_lengths, residual_rows, norm_gain,
            w_gate_up, w_down, expert_ids, gate_weights,
        )
    attention = attention_layer(queries, fresh_kv, kv_cache, selection, ctx_lengths)
    expert_out = expert_layer(residual_rows, norm_gain, w_gate_up, w_down, expert_ids, gate_weights)
    return (attention, expert_out)


def solution(mesh):
    return jax.shard_map(
        shards,
        mesh=mesh,
        in_specs=(
            P(("group", "ctx"), None),
            P(("group", "ctx"), None),
            P(("group", "ctx"), None, None),
            P("group", None),
            P("group"),
            P(("group", "ctx"), None),
            P(),
            P("ctx", None, None),
            P("ctx", None, None),
            P(("group", "ctx"), None),
            P(("group", "ctx"), None),
        ),
        out_specs=(P(("group", "ctx"), None), P(("group", "ctx"), None)),
        check_vma=False,
    )
```
